32 devices in a mesh: queue: 8 (over z, y), mp: 4 (over x, core).
Axes of the slice: x: 2, y: 2, z: 4, core: 2. Of those that a mesh axis runs over, the one named last changes fastest.
Arguments:
- state: bfloat16 [8, 512, 3072], P('queue', None, 'mp')
- key_cache: bfloat16 [8, 32, 3072], P('queue', None, 'mp'), as said below
- value_cache: bfloat16 [8, 32, 3072], P('queue', None, 'mp'), may hold values from -15 to 15
- level_gain: float32 [50, 3072], P(None, 'mp'), may hold values from 0.25 to 1.75
- sigma: float32 [51], replicated, may hold values from 0.05 to 1.5
- levels: int32 [8], P('queue'), may hold values from 0 to 49
- group_len: int32 [8], replicated, may hold values from 256 to 512, as said below
- ctx_ids: int32 [8, 6], P('queue'), may hold values from 0 to 6, as said below
- ctx_count: int32 [8], P('queue'), may hold values from 0 to 6, as said below
Outputs:
- advanced: bfloat16 [8, 512, 3072], P('queue', None, 'mp')
The draws below stay inside these ranges and needn't reach their ends.
Inputs may be any that keep to these rules, and one draw needn't show every extreme that they name: `group_len`: some group has exactly 512 live tokens. `ctx_count`: slot c lists at most min(c, 6) blocks, and the last slot lists exactly 6. `ctx_ids`: the first ctx_count[c] entries of slot c are distinct blocks of index below c; the other entries are 0. `key_cache`: keys of the clean context blocks.
All inputs are finite; a program needn't handle non-finite values.
Results may differ from the reference program's by a relative error of at most 0.015.
The reference program's roundings to bfloat16 on the way (of `current`, `queries`, `own_keys`, `rounded` and `updated`) count: a program that leaves them out, or rounds other values in their place, can miss the bound.
Values may be sent and summed in bfloat16 or wider, within the bound.
No kernel may reach another device: no remote copies, remote signals or barrier semaphores. Data moves between devices by JAX's collectives and lax.ppermute only.
A program may use at most 64 MiB of HBM per device.

```python
import math
import jax
import jax.numpy as jnp
from jax import lax

HEADS = 24
HEAD_DIM = 128
FEAT = 3072
CT = 512
CB = 32
NB = 6
LEVELS = 50
STEPS = 2
GROUPS = 8


def draw_state(key, part):
    first_key, second_key, third_key = jax.random.split(key, 3)
    shape_all = (GROUPS, CT, FEAT)
    base_draw = jax.random.normal(first_key, shape_all, jnp.float32)
    feature_index = jnp.arange(FEAT).astype(jnp.float32)
    column_scale = jnp.exp(0.5 * math.log(3.0) * (feature_index / FEAT - 0.5))
    column_scale = column_scale * jnp.exp(jax.random.uniform(second_key, (FEAT,), jnp.float32, -1.15, 1.15))
    row_scale = jnp.exp(jax.random.uniform(third_key, (GROUPS, CT, 1), jnp.float32, -1.15, 1.15))
    drawn = 0.3 * base_draw * column_scale * row_scale
    return drawn.astype(jnp.bfloat16)


def draw_key_cache(key, part):
    shape_all = (GROUPS, CB, FEAT)
    drawn = jax.random.normal(key, shape_all, jnp.float32)
    return drawn.astype(jnp.bfloat16)


def draw_group_len(key, part):
    first_key, second_key = jax.random.split(key, 2)
    lengths = jax.random.randint(first_key, (GROUPS,), CT // 2, CT + 1)
    fullest = jax.random.randint(second_key, (), 0, GROUPS)
    return jnp.where(jnp.arange(GROUPS) == fullest, CT, lengths).astype(jnp.int32)


def context_counts(key):
    slot_index = jnp.arange(GROUPS)
    wanted = jax.random.randint(jax.random.fold_in(key, 11), (GROUPS,), 1, NB + 1)
    counts = jnp.minimum(slot_index, wanted)
    return jnp.where(slot_index == GROUPS - 1, NB, counts).astype(jnp.int32)


def draw_ctx_count(key, part):
    return context_counts(key)


def draw_ctx_ids(key, part):
    counts = context_counts(key)
    raw_priority = jax.random.randint(jax.random.fold_in(key, 12), (GROUPS, GROUPS), 0, GROUPS)
    slot_index = jnp.arange(GROUPS)[:, None]
    block_index = jnp.arange(GROUPS)[None, :]
    priority = raw_priority + (GROUPS - block_index) // 2 + 2 * GROUPS * (block_index == slot_index - 1)
    priority = jnp.where(block_index < slot_index, priority, -1)
    priority = priority * GROUPS + block_index
    unused, picked = lax.top_k(priority, NB)
    listed = jnp.where(jnp.arange(NB)[None, :] < counts[:, None], picked, 0)
    return listed.astype(jnp.int32)


def plant(array, rng, smallest, top_value):
    spot = [jax.random.randint(jax.random.fold_in(rng, axis), (), 0, length) for axis, length in enumerate(array.shape)]
    widest = array.shape.index(max(array.shape))
    beside = spot[:widest] + [(spot[widest] + 1) % array.shape[widest]] + spot[widest + 1:]
    return array.at[tuple(spot)].set(smallest).at[tuple(beside)].set(top_value)


def block_scale(stream_key, dims, cuts, smallest, high):
    def one(position, blocks):
        steps = jax.random.uniform(jax.random.fold_in(jax.random.fold_in(stream_key, 6), position), (blocks,), jnp.float32, smallest / len(cuts), high / len(cuts))
        return jnp.repeat(jnp.exp(steps), dims[position] // blocks).reshape((-1,) + (1,) * (len(dims) - position - 1))

    loudness = one(*cuts[0])
    for cut in cuts[1:]:
        loudness = loudness * one(*cut)
    return loudness


def centred(rng, dims, scale, reach, shards=(), kind=jnp.bfloat16):
    values = jax.random.normal(rng, dims, jnp.float32) * scale
    if len(shards) > 0:
        values = block_scale(rng, dims, shards, -0.22, 0.18) * values
    return jnp.clip(values, min=-reach, max=reach).astype(kind)


def setup_inputs(seed: int = 0) -> dict:
    keys = jax.random.split(jax.random.key(seed), 10)
    return {
        "state": draw_state(jax.random.fold_in(keys[9], 71), 0),
        "key_cache": draw_key_cache(jax.random.fold_in(keys[9], 71), 0),
        "value_cache": centred(keys[2], (GROUPS, CB, FEAT), 2.5, 15.0, ((0, 8), (2, 4))),
        "level_gain": jnp.clip(1.0 + 0.15 * jax.random.normal(keys[3], (LEVELS, FEAT), jnp.float32), 0.25, 1.75),
        "sigma": jnp.clip(jnp.exp(jax.random.uniform(keys[4], (LEVELS + 1,), jnp.float32, math.log(0.05), math.log(1.5))), 0.05, 1.5),
        "levels": plant(jax.random.randint(keys[5], (GROUPS,), 0, LEVELS), jax.random.fold_in(keys[5], 1), 0, LEVELS - 1).astype(jnp.int32),
        "group_len": draw_group_len(jax.random.fold_in(keys[9], 71), 0),
        "ctx_ids": draw_ctx_ids(jax.random.fold_in(keys[9], 71), 0),
        "ctx_count": draw_ctx_count(jax.random.fold_in(keys[9], 71), 0),
    }


def attend(queries, all_keys, all_values, key_live, scaling):
    scores = jnp.einsum('rhd,khd->hrk', queries.astype(jnp.float32), all_keys.astype(jnp.float32)) * scaling
    scores = jnp.where(key_live[None, None, :], scores, -jnp.inf)
    row_max = lax.optimization_barrier(jnp.max(scores, axis=-1, keepdims=True))
    weights = jnp.exp(scores - row_max)
    totals = lax.optimization_barrier(jnp.sum(weights, axis=-1))
    rounded = weights.astype(jnp.bfloat16)
    weighted = jnp.einsum('hrk,khd->rhd', rounded.astype(jnp.float32), all_values.astype(jnp.float32))
    return weighted / jnp.transpose(totals)[:, :, None]

def reference(state, key_cache, value_cache, level_gain, sigma, levels, group_len, ctx_ids, ctx_count):
    row_count = state.shape[1]
    scaling = HEAD_DIM ** (-0.5)
    step_sizes = sigma[levels + 1] - sigma[levels]
    level_gains = level_gain[levels]
    current = state
    for step_index in range(STEPS):
        lengths = jnp.roll(group_len, step_index)
        widened = current.astype(jnp.float32)
        mean_square = lax.optimization_barrier(jnp.mean(widened * widened, axis=-1, keepdims=True))
        normed = widened * lax.rsqrt(mean_square + 1e-06)
        queries = (normed * level_gains[:, None, :]).astype(jnp.bfloat16)
        own_keys = normed.astype(jnp.bfloat16)

        def per_group(inputs):
            query_rows, key_rows, own_values, block_list, list_count, length, step_size = inputs
            context_keys = key_cache[block_list].reshape(NB * CB, FEAT)
            context_values = value_cache[block_list].reshape(NB * CB, FEAT)
            all_keys = jnp.concatenate([key_rows, context_keys], axis=0)
            all_values = jnp.concatenate([own_values, context_values], axis=0)
            token_live = jnp.arange(row_count) < length
            block_live = jnp.repeat(jnp.arange(NB) < list_count, CB)
            key_live = jnp.concatenate([token_live, block_live], axis=0)
            attended = attend(query_rows.reshape(row_count, HEADS, HEAD_DIM), all_keys.reshape(-1, HEADS, HEAD_DIM), all_values.reshape(-1, HEADS, HEAD_DIM), key_live, scaling)
            attended = attended.reshape(row_count, FEAT)
            widened_own = own_values.astype(jnp.float32)
            advanced_rows = jnp.where(token_live[:, None], widened_own + step_size * attended, widened_own)
            return advanced_rows.astype(jnp.bfloat16)
        updated = lax.map(per_group, (queries, own_keys, current, ctx_ids, ctx_count, lengths, step_sizes))
        current = jnp.roll(updated, 1, axis=0)
    return current
```

```python
import functools
import math

import jax
import jax.numpy as jnp
from jax import lax
from jax.experimental import pallas as pl
from jax.experimental.pallas import tpu as pltpu
from jax.sharding import PartitionSpec as P

HEAD_DIM = 128
FEAT = 3072
STEPS = 2
CHUNKS = 3
ROWS = 128
NEG = -1e30


def shifted(array, by):
    peers = lax.axis_size("queue")
    return lax.ppermute(array, "queue", [(i, (i + by) % peers) for i in range(peers)])


def crossed(array, stride):
    peers = lax.axis_size("queue")
    return lax.ppermute(array, "queue", [(i, i ^ stride) for i in range(peers)])


def row_sums(squares):
    return jnp.sum(squares.T, axis=0, keepdims=True)


def prepare_kernel(levels, ctx_ids, ctx_count, state, keys, values, *outs):
    chunks, (cache, sums, facts) = outs[:CHUNKS], outs[CHUNKS:]
    rows, block_rows = state.shape[1], keys.shape[1]
    width = chunks[0].shape[1]
    listed = ctx_ids.shape[1]
    cache[:block_rows, :] = keys[0]
    cache[block_rows:, :] = values[0]
    squares = jnp.zeros((rows, HEAD_DIM), jnp.float32)
    for c, chunk in enumerate(chunks):
        chunk[...] = state[0, :, c * width : (c + 1) * width]
        for h in range(width // HEAD_DIM):
            start = c * width + h * HEAD_DIM
            x = state[0, :, start : start + HEAD_DIM].astype(jnp.float32)
            squares += x * x
    sums[:, :rows] = row_sums(squares)
    lane = lax.broadcasted_iota(jnp.int32, (1, HEAD_DIM), 1)
    packed = jnp.where(lane == 0, levels[0], 0) + jnp.where(lane == 1, ctx_count[0], 0)
    facts[0, 0] = levels[0]
    facts[0, 1] = ctx_count[0]
    for k in range(listed):
        packed += jnp.where(lane == 2 + k, ctx_ids[0, k], 0)
        facts[0, 2 + k] = ctx_ids[0, k]
    first = lax.axis_index("mp") == 0
    sums[:, rows:] = jnp.where(first, packed, 0).astype(jnp.float32)


def step_kernel(
    facts, sigma, group_len, sums, level_gain, *rest, chunk_count, sources, first_head, last, listed, base
):
    chunks, rest = rest[:chunk_count], rest[chunk_count:]
    caches, rest = rest[: len(sources)], rest[len(sources) :]
    if last:
        (out,), rest = rest[:1], rest[1:]
    else:
        outs, partial, rest = rest[:chunk_count], rest[chunk_count], rest[chunk_count + 1 :]
    keys, values, spread = rest
    rows, width = chunks[0].shape
    slots = group_len.shape[0]
    slot = lax.axis_index("queue")
    level = facts[0, base].astype(jnp.int32)
    count = facts[0, base + 1].astype(jnp.int32)
    step_size = sigma[level + 1] - sigma[level]
    length = group_len[lax.rem(slot - STEPS + slots, slots)]
    total = keys.shape[0]
    block_rows = (total - rows) // slots

    level_row = lax.broadcasted_iota(jnp.int32, (level_gain.shape[0], HEAD_DIM), 0)
    column = lax.broadcasted_iota(jnp.int32, (1, total), 1)
    relative = (column - rows) // block_rows
    live = column < length
    for k in range(listed):
        block = jnp.where(k < count, facts[0, base + 2 + k].astype(jnp.int32) ^ slot, slots)
        live = jnp.logical_or(live, jnp.logical_and(column >= rows, relative == block))

    scale = lax.rsqrt(sums[:, :rows] / FEAT + 1e-06)
    spread[...] = jnp.broadcast_to(scale, (HEAD_DIM, rows)).T
    rate = math.log2(math.e) * HEAD_DIM**-0.5
    squares = [jnp.zeros((ROWS, HEAD_DIM), jnp.float32) for _ in range(rows // ROWS)]
    for c in range(chunk_count):
        for h in range(width // HEAD_DIM):
            inside = slice(h * HEAD_DIM, (h + 1) * HEAD_DIM)
            start = (first_head + c * (width // HEAD_DIM) + h) * HEAD_DIM
            across = slice(start, start + HEAD_DIM)
            gain = jnp.sum(jnp.where(level_row == level, level_gain[:, across], 0.0), axis=0, keepdims=True)
            x_all = chunks[c][:, inside]
            keys[:rows, :] = (x_all.astype(jnp.float32) * spread[...]).astype(jnp.bfloat16)
            values[:rows, :] = x_all
            for cache, blocks in zip(caches, sources):
                for j, block in enumerate(blocks):
                    base = 2 * block_rows * j
                    into = slice(rows + block * block_rows, rows + (block + 1) * block_rows)
                    keys[into, :] = cache[base : base + block_rows, across]
                    values[into, :] = cache[base + block_rows : base + 2 * block_rows, across]
            for r in range(rows // ROWS):
                here = slice(r * ROWS, (r + 1) * ROWS)
                x = chunks[c][here, inside].astype(jnp.float32)
                query = (x * spread[here, :] * gain).astype(jnp.bfloat16)
                scores = lax.dot_general(
                    query, keys[...], (((1,), (1,)), ((), ())), preferred_element_type=jnp.float32
                )
                scores = jnp.where(live, scores, NEG)
                peak = jnp.max(scores, axis=1, keepdims=True)
                weights = jnp.exp2((scores - peak) * rate)
                mass = jnp.sum(weights, axis=1, keepdims=True)
                mixed = jnp.dot(
                    weights.astype(jnp.bfloat16), values[...], preferred_element_type=jnp.float32
                )
                row = lax.broadcasted_iota(jnp.int32, (ROWS, HEAD_DIM), 0) + r * ROWS
                moved = jnp.where(row < length, x + step_size * (mixed / mass), x)
                updated = moved.astype(jnp.bfloat16)
                if last:
                    out[0, here, across] = updated
                else:
                    outs[c][here, inside] = updated
                    wide = updated.astype(jnp.float32)
                    squares[r] += wide * wide
    if not last:
        partial[...] = jnp.concatenate([row_sums(s) for s in squares], axis=1)


def on_device(
    state, key_cache, value_cache, level_gain, sigma, levels, group_len, ctx_ids, ctx_count
):
    rows, features = state.shape[1:]
    block_rows = key_cache.shape[1]
    slots = lax.axis_size("queue")
    listed = ctx_ids.shape[1]
    width = features // CHUNKS
    vmem = pl.BlockSpec(memory_space=pltpu.VMEM)
    smem = pl.BlockSpec(memory_space=pltpu.SMEM)

    *chunks, cache, sums, facts = pl.pallas_call(
        prepare_kernel,
        out_shape=[jax.ShapeDtypeStruct((rows, width), state.dtype)] * CHUNKS
        + [
            jax.ShapeDtypeStruct((2 * block_rows, features), key_cache.dtype),
            jax.ShapeDtypeStruct((1, rows + HEAD_DIM), jnp.float32),
            jax.ShapeDtypeStruct((1, 2 + listed), jnp.int32),
        ],
        in_specs=[smem] * 3 + [vmem] * 3,
        out_specs=[vmem] * (CHUNKS + 2) + [smem],
        name="prepare",
    )(levels, ctx_ids, ctx_count, state, key_cache, value_cache)

    arrivals = [(cache, (0,))]
    stride = slots // 2
    while stride > 1:
        payload = [a for a, _ in arrivals]
        blocks = tuple(stride ^ b for _, bs in arrivals for b in bs)
        payload = payload[0] if len(payload) == 1 else jnp.concatenate(payload, axis=0)
        arrivals.append((crossed(payload, stride), blocks))
        stride //= 2
    arrivals += [(crossed(a, 1), tuple(1 ^ b for b in bs)) for a, bs in arrivals]
    caches = [a for a, _ in arrivals]
    sources = tuple(bs for _, bs in arrivals)

    reduced = lax.psum(sums, "mp")
    first_facts = shifted(reduced, STEPS)
    second_facts = shifted(facts, STEPS - 1)
    landed = [shifted(chunk, STEPS) for chunk in chunks]

    def step(facts_in, sums_in, parts, first_head, last):
        heads = len(parts) * width // HEAD_DIM
        total = rows + slots * block_rows
        if last:
            out_shape = [jax.ShapeDtypeStruct((1, rows, features), state.dtype)]
        else:
            out_shape = [jax.ShapeDtypeStruct(p.shape, p.dtype) for p in parts]
            out_shape += [jax.ShapeDtypeStruct((1, rows), jnp.float32)]
        return pl.pallas_call(
            functools.partial(
                step_kernel,
                chunk_count=len(parts),
                sources=sources,
                first_head=first_head,
                last=last,
                listed=listed,
                base=0 if last else rows,
            ),
            out_shape=out_shape,
            in_specs=[smem] * 3 + [vmem] * (2 + len(parts) + len(caches)),
            out_specs=[vmem] * len(out_shape),
            scratch_shapes=[
                pltpu.VMEM((total, HEAD_DIM), jnp.bfloat16),
                pltpu.VMEM((total, HEAD_DIM), jnp.bfloat16),
                pltpu.VMEM((rows, HEAD_DIM), jnp.float32),
            ],
            cost_estimate=pl.CostEstimate(
                flops=4 * heads * rows * total * HEAD_DIM,
                bytes_accessed=4 * heads * rows * HEAD_DIM,
                transcendentals=heads * rows * total,
            ),
            name="denoise",
        )(facts_in, sigma, group_len, sums_in, level_gain, *parts, *caches)

    moved, partials = [], []
    for c, part in enumerate(landed):
        new, partial = step(first_facts, first_facts, [part], c * width // HEAD_DIM, False)
        moved.append(new)
        partials.append(partial)
    second_sums = lax.psum(functools.reduce(jnp.add, partials), "mp")
    (out,) = step(second_facts, second_sums, moved, 0, True)
    return out


def solution(mesh):
    in_specs = (
        P("queue", None, "mp"),
        P("queue", None, "mp"),
        P("queue", None, "mp"),
        P(None, "mp"),
        P(),
        P("queue"),
        P(),
        P("queue", None),
        P("queue"),
    )
    out_specs = P("queue", None, "mp")
    return jax.shard_map(
        on_device, mesh=mesh, in_specs=in_specs, out_specs=out_specs, check_vma=False
    )
```

```python
import functools
import math

import jax
import jax.numpy as jnp
from jax import lax
from jax.experimental import pallas as pl
from jax.experimental.pallas import tpu as pltpu
from jax.sharding import PartitionSpec as P

HEAD_DIM = 128
FEAT = 3072
STEPS = 2
CHUNKS = 3
ROWS = 256
NEG = -1e30


def shifted(array, by):
    peers = lax.axis_size("queue")
    return lax.ppermute(array, "queue", [(i, (i + by) % peers) for i in range(peers)])


def crossed(array, stride):
    peers = lax.axis_size("queue")
    return lax.ppermute(array, "queue", [(i, i ^ stride) for i in range(peers)])


def row_sums(squares):
    return jnp.sum(squares.T, axis=0, keepdims=True)


def prepare_kernel(levels, ctx_ids, ctx_count, state, keys, values, *outs):
    chunks, (cache, sums, facts) = outs[:CHUNKS], outs[CHUNKS:]
    rows, block_rows = state.shape[1], keys.shape[1]
    width = chunks[0].shape[1]
    listed = ctx_ids.shape[1]
    cache[:block_rows, :] = keys[0]
    cache[block_rows:, :] = values[0]
    squares = jnp.zeros((rows, HEAD_DIM), jnp.float32)
    for c, chunk in enumerate(chunks):
        chunk[...] = state[0, :, c * width : (c + 1) * width]
        for h in range(width // HEAD_DIM):
            start = c * width + h * HEAD_DIM
            x = state[0, :, start : start + HEAD_DIM].astype(jnp.float32)
            squares += x * x
    sums[:, :rows] = row_sums(squares)
    lane = lax.broadcasted_iota(jnp.int32, (1, HEAD_DIM), 1)
    packed = jnp.where(lane == 0, levels[0], 0) + jnp.where(lane == 1, ctx_count[0], 0)
    facts[0, 0] = levels[0]
    facts[0, 1] = ctx_count[0]
    for k in range(listed):
        packed += jnp.where(lane == 2 + k, ctx_ids[0, k], 0)
        facts[0, 2 + k] = ctx_ids[0, k]
    first = lax.axis_index("mp") == 0
    sums[:, rows:] = jnp.where(first, packed, 0).astype(jnp.float32)


def step_kernel(
    facts, sigma, group_len, sums, level_gain, *rest, chunk_count, sources, first_head, last, listed, base
):
    chunks, rest = rest[:chunk_count], rest[chunk_count:]
    caches, rest = rest[: len(sources)], rest[len(sources) :]
    if last:
        (out,), rest = rest[:1], rest[1:]
    else:
        outs, partial, rest = rest[:chunk_count], rest[chunk_count], rest[chunk_count + 1 :]
    keys, values, spread, scores = rest
    rows, width = chunks[0].shape
    slots = group_len.shape[0]
    slot = lax.axis_index("queue")
    level = facts[0, base].astype(jnp.int32)
    count = facts[0, base + 1].astype(jnp.int32)
    step_size = sigma[level + 1] - sigma[level]
    length = group_len[lax.rem(slot - STEPS + slots, slots)]
    total = keys.shape[1]
    block_rows = (total - rows) // slots
    chunk_heads = width // HEAD_DIM
    head_count = chunk_count * chunk_heads
    per_head = rows // ROWS
    rate = math.log2(math.e) * HEAD_DIM**-0.5

    level_row = lax.broadcasted_iota(jnp.int32, (level_gain.shape[0], HEAD_DIM), 0)
    token = lax.broadcasted_iota(jnp.int32, (rows, HEAD_DIM), 0)
    alive = token < length
    names = []
    for k in range(listed):
        names.append(jnp.where(k < count, facts[0, base + 2 + k].astype(jnp.int32) ^ slot, slots))
    listed_here = []
    for block in range(slots):
        found = names[0] == block
        for name in names[1:]:
            found = jnp.logical_or(found, name == block)
        listed_here.append(found)
    scale = lax.rsqrt(sums[:, :rows] / FEAT + 1e-06)
    spread[...] = jnp.where(alive, jnp.broadcast_to(scale, (HEAD_DIM, rows)).T, 0.0)
    for half in range(min(2, head_count)):
        values[half, :rows, HEAD_DIM:] = jnp.where(alive, 1.0, 0.0).astype(jnp.bfloat16)
        for block in range(slots):
            into = slice(rows + block * block_rows, rows + (block + 1) * block_rows)
            mark = jnp.where(listed_here[block], 1.0, 0.0)
            values[half, into, HEAD_DIM:] = jnp.full((block_rows, HEAD_DIM), mark).astype(jnp.bfloat16)

    def head_of(h):
        c, inside = h // chunk_heads, (h % chunk_heads) * HEAD_DIM
        start = (first_head + h) * HEAD_DIM
        return c, slice(inside, inside + HEAD_DIM), slice(start, start + HEAD_DIM)

    def lay(h):
        c, inside, across = head_of(h)
        half = h % 2
        x = chunks[c][:, inside]
        wide = x.astype(jnp.float32)
        keys[half, :rows, :] = (wide * spread[...]).astype(jnp.bfloat16)
        values[half, :rows, :HEAD_DIM] = jnp.where(alive, wide, 0.0).astype(jnp.bfloat16)
        for cache, blocks in zip(caches, sources):
            for j, block in enumerate(blocks):
                start = 2 * block_rows * j
                into = slice(rows + block * block_rows, rows + (block + 1) * block_rows)
                none = jnp.zeros((block_rows, HEAD_DIM), jnp.bfloat16)
                keys[half, into, :] = jnp.where(
                    listed_here[block], cache[start : start + block_rows, across], none
                )
                values[half, into, :HEAD_DIM] = jnp.where(
                    listed_here[block], cache[start + block_rows : start + 2 * block_rows, across], none
                )

    def score(t):
        h, r = divmod(t, per_head)
        if r == 0:
            lay(h)
        c, inside, across = head_of(h)
        here = slice(r * ROWS, (r + 1) * ROWS)
        gain = jnp.sum(jnp.where(level_row == level, level_gain[:, across], 0.0), axis=0, keepdims=True)
        query = (chunks[c][here, inside].astype(jnp.float32) * spread[here, :] * gain).astype(jnp.bfloat16)
        scores[t % 2] = lax.dot_general(
            query, keys[h % 2], (((1,), (1,)), ((), ())), preferred_element_type=jnp.float32
        )

    squares = [jnp.zeros((ROWS, HEAD_DIM), jnp.float32) for _ in range(per_head)]

    def mix(t):
        h, r = divmod(t, per_head)
        c, inside, across = head_of(h)
        here = slice(r * ROWS, (r + 1) * ROWS)
        s = scores[t % 2]
        peak = jnp.max(s, axis=1, keepdims=True)
        weights = jnp.exp2((s - peak) * rate).astype(jnp.bfloat16)
        mixed = jnp.dot(weights, values[h % 2], preferred_element_type=jnp.float32)
        x = chunks[c][here, inside].astype(jnp.float32)
        moved = x + step_size * (mixed[:, :HEAD_DIM] / mixed[:, HEAD_DIM:])
        updated = jnp.where(alive[here], moved, x).astype(jnp.bfloat16)
        if last:
            out[0, here, across] = updated
        else:
            outs[c][here, inside] = updated
            wide = updated.astype(jnp.float32)
            squares[r] += wide * wide

    tasks = head_count * per_head
    score(0)
    for t in range(tasks):
        if t + 1 < tasks:
            score(t + 1)
        mix(t)
    if not last:
        partial[...] = jnp.concatenate([row_sums(s) for s in squares], axis=1)


def denoise(
    facts, sigma, group_len, sums, level_gain, parts, caches, sources, first_head, last, listed
):
    vmem = pl.BlockSpec(memory_space=pltpu.VMEM)
    smem = pl.BlockSpec(memory_space=pltpu.SMEM)
    rows, width = parts[0].shape
    slots = group_len.shape[0]
    features = level_gain.shape[1]
    block_rows = sum(a.shape[0] for a in caches) // (2 * slots)
    heads = len(parts) * width // HEAD_DIM
    total = rows + slots * block_rows
    if last:
        out_shape = [jax.ShapeDtypeStruct((1, rows, features), parts[0].dtype)]
    else:
        out_shape = [jax.ShapeDtypeStruct(p.shape, p.dtype) for p in parts]
        out_shape += [jax.ShapeDtypeStruct((1, rows), jnp.float32)]
    return pl.pallas_call(
        functools.partial(
            step_kernel,
            chunk_count=len(parts),
            sources=sources,
            first_head=first_head,
            last=last,
            listed=listed,
            base=0 if last else rows,
        ),
        out_shape=out_shape,
        in_specs=[smem] * 3 + [vmem] * (2 + len(parts) + len(caches)),
        out_specs=[vmem] * len(out_shape),
        scratch_shapes=[
            pltpu.VMEM((2, total, HEAD_DIM), jnp.bfloat16),
            pltpu.VMEM((2, total, 2 * HEAD_DIM), jnp.bfloat16),
            pltpu.VMEM((rows, HEAD_DIM), jnp.float32),
            pltpu.VMEM((2, ROWS, total), jnp.float32),
        ],
        cost_estimate=pl.CostEstimate(
            flops=4 * heads * rows * total * HEAD_DIM,
            bytes_accessed=4 * heads * rows * HEAD_DIM,
            transcendentals=heads * rows * total,
        ),
        name="denoise",
    )(facts, sigma, group_len, sums, level_gain, *parts, *caches)


def on_device(
    state, key_cache, value_cache, level_gain, sigma, levels, group_len, ctx_ids, ctx_count
):
    rows, features = state.shape[1:]
    block_rows = key_cache.shape[1]
    slots = lax.axis_size("queue")
    listed = ctx_ids.shape[1]
    width = features // CHUNKS
    vmem = pl.BlockSpec(memory_space=pltpu.VMEM)
    smem = pl.BlockSpec(memory_space=pltpu.SMEM)

    *chunks, cache, sums, facts = pl.pallas_call(
        prepare_kernel,
        out_shape=[jax.ShapeDtypeStruct((rows, width), state.dtype)] * CHUNKS
        + [
            jax.ShapeDtypeStruct((2 * block_rows, features), key_cache.dtype),
            jax.ShapeDtypeStruct((1, rows + HEAD_DIM), jnp.float32),
            jax.ShapeDtypeStruct((1, 2 + listed), jnp.int32),
        ],
        in_specs=[smem] * 3 + [vmem] * 3,
        out_specs=[vmem] * (CHUNKS + 2) + [smem],
        name="prepare",
    )(levels, ctx_ids, ctx_count, state, key_cache, value_cache)

    arrivals = [(cache, (0,))]
    stride = slots // 2
    while stride > 1:
        payload = [a for a, _ in arrivals]
        blocks = tuple(stride ^ b for _, bs in arrivals for b in bs)
        payload = payload[0] if len(payload) == 1 else jnp.concatenate(payload, axis=0)
        arrivals.append((crossed(payload, stride), blocks))
        stride //= 2
    arrivals += [(crossed(a, 1), tuple(1 ^ b for b in bs)) for a, bs in arrivals]
    caches = [a for a, _ in arrivals]
    sources = tuple(bs for _, bs in arrivals)

    reduced = lax.psum(sums, "mp")
    first_facts = shifted(reduced, STEPS)
    second_facts = shifted(facts, STEPS - 1)
    landed = [shifted(chunk, STEPS) for chunk in chunks]

    moved, partials = [], []
    for c, part in enumerate(landed):
        new, partial = denoise(
            first_facts, sigma, group_len, first_facts, level_gain, [part], caches, sources,
            c * width // HEAD_DIM, False, listed,
        )
        moved.append(new)
        partials.append(partial)
    second_sums = lax.psum(functools.reduce(jnp.add, partials), "mp")
    (out,) = denoise(
        second_facts, sigma, group_len, second_sums, level_gain, moved, caches, sources, 0, True, listed
    )
    return out


def solution(mesh):
    in_specs = (
        P("queue", None, "mp"),
        P("queue", None, "mp"),
        P("queue", None, "mp"),
        P(None, "mp"),
        P(),
        P("queue"),
        P(),
        P("queue", None),
        P("queue"),
    )
    out_specs = P("queue", None, "mp")
    return jax.shard_map(
        on_device, mesh=mesh, in_specs=in_specs, out_specs=out_specs, check_vma=False
    )
```

```python
import functools
import math

import jax
import jax.numpy as jnp
from jax import lax
from jax.experimental import pallas as pl
from jax.experimental.pallas import tpu as pltpu
from jax.sharding import PartitionSpec as P


HEAD_DIM = 128
FEAT = 3072
STEPS = 2
ROWS = 256
MIB = 1024 * 1024


def shifted(array, by):
    peers = lax.axis_size("queue")
    return lax.ppermute(array, "queue", [(i, (i + by) % peers) for i in range(peers)])


def crossed(array, stride, axis):
    return lax.ppermute(array, axis, [(i, i ^ stride) for i in range(lax.axis_size(axis))])


def listable(slots):
    found = []
    for place in range(slots):
        group = (place - STEPS) % slots
        entered = [(group + step) % slots for step in range(STEPS)]
        found.append(set(range(max(entered))))
    return found


def row_sums(squares):
    return jnp.sum(squares.T, axis=0, keepdims=True)


def cut_kernel(levels, ctx_count, ctx_ids, keys, values, state, cache, packed, facts, *rest):
    *chunks, ids, arrived = rest
    block_rows = keys.shape[1]
    copies = [
        pltpu.make_async_copy(keys.at[0], cache.at[:block_rows], arrived.at[0]),
        pltpu.make_async_copy(values.at[0], cache.at[block_rows:], arrived.at[1]),
        pltpu.make_async_copy(ctx_ids, ids, arrived.at[2]),
    ]
    start = 0
    for c, chunk in enumerate(chunks):
        width = chunk.shape[1]
        copies.append(
            pltpu.make_async_copy(state.at[0, :, start : start + width], chunk, arrived.at[3 + c])
        )
        start += width
    for copy in copies:
        copy.start()
    for copy in copies:
        copy.wait()
    lane = lax.broadcasted_iota(jnp.int32, (1, HEAD_DIM), 1)
    row = jnp.where(lane == 0, levels[0], 0) + jnp.where(lane == 1, ctx_count[0], 0)
    facts[0, 0] = levels[0]
    facts[0, 1] = ctx_count[0]
    for k in range(ids.shape[1]):
        row += jnp.where(lane == 2 + k, ids[0, k], 0)
        facts[0, 2 + k] = ids[0, k]
    first = lax.axis_index("mp") == 0
    packed[...] = jnp.where(first, row, 0).astype(jnp.float32)


def sums_kernel(packed, *refs):
    *chunks, sums = refs
    rows = chunks[0].shape[0]
    squares = jnp.zeros((rows, HEAD_DIM), jnp.float32)
    for chunk in chunks:
        for h in range(chunk.shape[1] // HEAD_DIM):
            x = chunk[:, h * HEAD_DIM : (h + 1) * HEAD_DIM].astype(jnp.float32)
            squares += x * x
    sums[:, :rows] = row_sums(squares)
    sums[:, rows:] = packed[...]


def step_kernel(
    facts, sigma, group_len, sums, level_gain, *rest, chunk_count, sources, first_head, last, listed, base, chained
):
    chunks, rest = rest[:chunk_count], rest[chunk_count:]
    caches, rest = rest[: len(sources)], rest[len(sources) :]
    if chained:
        earlier, rest = rest[0], rest[1:]
    if last:
        (out,), rest = rest[:1], rest[1:]
    else:
        outs, partial, rest = rest[:chunk_count], rest[chunk_count], rest[chunk_count + 1 :]
    keys, values, spread, scores = rest
    rows = chunks[0].shape[0]
    slots = group_len.shape[0]
    slot = lax.axis_index("queue")
    level = facts[0, base].astype(jnp.int32)
    count = facts[0, base + 1].astype(jnp.int32)
    step_size = sigma[level + 1] - sigma[level]
    length = group_len[lax.rem(slot - STEPS + slots, slots)]
    total = keys.shape[1]
    block_rows = (total - rows) // slots
    places = [(c, j) for c in range(chunk_count) for j in range(chunks[c].shape[1] // HEAD_DIM)]
    head_count = len(places)
    per_head = rows // ROWS
    rate = math.log2(math.e) * HEAD_DIM**-0.5

    level_row = lax.broadcasted_iota(jnp.int32, (level_gain.shape[0], HEAD_DIM), 0)
    token = lax.broadcasted_iota(jnp.int32, (rows, HEAD_DIM), 0)
    alive = token < length
    order = [source for blocks in sources for source in blocks]
    listed_here = []
    for flip, back in order:
        block = lax.rem((slot ^ flip) - back + slots, slots)
        found = jnp.logical_and(count > 0, facts[0, base + 2].astype(jnp.int32) == block)
        for k in range(1, listed):
            same = facts[0, base + 2 + k].astype(jnp.int32) == block
            found = jnp.logical_or(found, jnp.logical_and(count > k, same))
        listed_here.append(found)
    scale = lax.rsqrt(sums[:, :rows] / FEAT + 1e-06)
    spread[...] = jnp.where(alive, jnp.broadcast_to(scale, (HEAD_DIM, rows)).T, 0.0)
    for half in range(min(2, head_count)):
        values[half, :rows, HEAD_DIM:] = jnp.where(alive, 1.0, 0.0).astype(jnp.bfloat16)
        for block in range(slots):
            into = slice(rows + block * block_rows, rows + (block + 1) * block_rows)
            mark = jnp.where(listed_here[block], 1.0, 0.0)
            values[half, into, HEAD_DIM:] = jnp.full((block_rows, HEAD_DIM), mark).astype(jnp.bfloat16)

    def head_of(h):
        c, inside = places[h][0], places[h][1] * HEAD_DIM
        start = (first_head + h) * HEAD_DIM
        return c, slice(inside, inside + HEAD_DIM), slice(start, start + HEAD_DIM)

    def lay(h):
        c, inside, across = head_of(h)
        half = h % 2
        x = chunks[c][:, inside]
        wide = x.astype(jnp.float32)
        keys[half, :rows, :] = (wide * spread[...]).astype(jnp.bfloat16)
        values[half, :rows, :HEAD_DIM] = jnp.where(alive, wide, 0.0).astype(jnp.bfloat16)
        block = -1
        for cache, blocks in zip(caches, sources):
            for j in range(len(blocks)):
                block += 1
                start = 2 * block_rows * j
                into = slice(rows + block * block_rows, rows + (block + 1) * block_rows)
                none = jnp.zeros((block_rows, HEAD_DIM), jnp.bfloat16)
                keys[half, into, :] = jnp.where(
                    listed_here[block], cache[start : start + block_rows, across], none
                )
                values[half, into, :HEAD_DIM] = jnp.where(
                    listed_here[block], cache[start + block_rows : start + 2 * block_rows, across], none
                )

    def score(t):
        h, r = divmod(t, per_head)
        if r == 0:
            lay(h)
        c, inside, across = head_of(h)
        here = slice(r * ROWS, (r + 1) * ROWS)
        gain = jnp.sum(jnp.where(level_row == level, level_gain[:, across], 0.0), axis=0, keepdims=True)
        query = (chunks[c][here, inside].astype(jnp.float32) * spread[here, :] * gain).astype(jnp.bfloat16)
        scores[t % 2] = lax.dot_general(
            query, keys[h % 2], (((1,), (1,)), ((), ())), preferred_element_type=jnp.float32
        )

    squares = [jnp.zeros((ROWS, HEAD_DIM), jnp.float32) for _ in range(per_head)]

    def mix(t):
        h, r = divmod(t, per_head)
        c, inside, across = head_of(h)
        here = slice(r * ROWS, (r + 1) * ROWS)
        s = scores[t % 2]
        peak = jnp.max(s, axis=1, keepdims=True)
        weights = jnp.exp2((s - peak) * rate).astype(jnp.bfloat16)
        mixed = jnp.dot(weights, values[h % 2], preferred_element_type=jnp.float32)
        x = chunks[c][here, inside].astype(jnp.float32)
        moved = x + step_size * (mixed[:, :HEAD_DIM] / mixed[:, HEAD_DIM:])
        updated = jnp.where(alive[here], moved, x).astype(jnp.bfloat16)
        if last:
            out[0, here, across] = updated
        else:
            outs[c][here, inside] = updated
            wide = updated.astype(jnp.float32)
            squares[r] += wide * wide

    tasks = head_count * per_head
    score(0)
    for t in range(tasks):
        if t + 1 < tasks:
            score(t + 1)
        mix(t)
    if not last:
        added = jnp.concatenate([row_sums(s) for s in squares], axis=1)
        partial[...] = added + earlier[...] if chained else added


def denoise(
    facts, sigma, group_len, sums, level_gain, parts, caches, sources, first_head, last, listed, earlier=()
):
    vmem = pl.BlockSpec(memory_space=pltpu.VMEM)
    smem = pl.BlockSpec(memory_space=pltpu.SMEM)
    rows = parts[0].shape[0]
    slots = group_len.shape[0]
    features = level_gain.shape[1]
    block_rows = sum(a.shape[0] for a in caches) // (2 * slots)
    heads = sum(p.shape[1] for p in parts) // HEAD_DIM
    total = rows + slots * block_rows
    if last:
        out_shape = [jax.ShapeDtypeStruct((1, rows, features), parts[0].dtype)]
    else:
        out_shape = [jax.ShapeDtypeStruct(p.shape, p.dtype) for p in parts]
        out_shape += [jax.ShapeDtypeStruct((1, rows), jnp.float32)]
    return pl.pallas_call(
        functools.partial(
            step_kernel,
            chunk_count=len(parts),
            sources=sources,
            first_head=first_head,
            last=last,
            listed=listed,
            base=0 if last else rows,
            chained=len(earlier) > 0,
        ),
        out_shape=out_shape,
        in_specs=[smem] * 3 + [vmem] * (2 + len(parts) + len(caches) + len(earlier)),
        out_specs=[vmem] * len(out_shape),
        scratch_shapes=[
            pltpu.VMEM((2, total, HEAD_DIM), jnp.bfloat16),
            pltpu.VMEM((2, total, 2 * HEAD_DIM), jnp.bfloat16),
            pltpu.VMEM((rows, HEAD_DIM), jnp.float32),
            pltpu.VMEM((2, ROWS, total), jnp.float32),
        ],
        cost_estimate=pl.CostEstimate(
            flops=4 * heads * rows * total * HEAD_DIM,
            bytes_accessed=4 * heads * rows * HEAD_DIM,
            transcendentals=heads * rows * total,
        ),
        compiler_params=pltpu.CompilerParams(vmem_limit_bytes=8 * MIB + 4 * total * (ROWS * 4 + 2 * features)),
        name="denoise",
    )(facts, sigma, group_len, sums, level_gain, *parts, *caches, *earlier)


def chunk_heads(heads):
    sizes = [1]
    while sum(sizes) < heads:
        sizes.append(min(2, heads - sum(sizes)))
    return sizes


def on_device(
    state, key_cache, value_cache, level_gain, sigma, levels, group_len, ctx_ids, ctx_count
):
    rows, features = state.shape[1:]
    block_rows = key_cache.shape[1]
    slots = lax.axis_size("queue")
    listed = ctx_ids.shape[1]
    sizes = chunk_heads(features // HEAD_DIM)
    vmem = pl.BlockSpec(memory_space=pltpu.VMEM)
    smem = pl.BlockSpec(memory_space=pltpu.SMEM)
    small = pltpu.CompilerParams(vmem_limit_bytes=8 * MIB)

    in_hbm = [
        pltpu.with_memory_space_constraint(a, pltpu.HBM)
        for a in (ctx_ids, key_cache, value_cache, state)
    ]
    cache, packed, facts, *chunks = pl.pallas_call(
        cut_kernel,
        out_shape=[
            jax.ShapeDtypeStruct((2 * block_rows, features), key_cache.dtype),
            jax.ShapeDtypeStruct((1, HEAD_DIM), jnp.float32),
            jax.ShapeDtypeStruct((1, 2 + listed), jnp.int32),
        ]
        + [jax.ShapeDtypeStruct((rows, n * HEAD_DIM), state.dtype) for n in sizes],
        in_specs=[smem] * 2 + [pl.BlockSpec(memory_space=pltpu.HBM)] * 4,
        out_specs=[vmem] * 2 + [smem] + [vmem] * len(sizes),
        scratch_shapes=[
            pltpu.SMEM((1, listed), jnp.int32),
            pltpu.SemaphoreType.DMA((3 + len(sizes),)),
        ],
        compiler_params=small,
        name="cut",
    )(levels, ctx_count, *in_hbm)
    sums = pl.pallas_call(
        sums_kernel,
        out_shape=jax.ShapeDtypeStruct((1, rows + HEAD_DIM), jnp.float32),
        in_specs=[vmem] * (1 + len(sizes)),
        out_specs=vmem,
        compiler_params=small,
        name="sums",
    )(packed, *chunks)

    needed = listable(slots)
    far, backs = [], []
    for i in range(slots // STEPS - 1):
        by = STEPS * (i + 1)
        pairs = [(p, (p + by) % slots) for p in range(slots)]
        pairs = [(p, q) for p, q in pairs if p in needed[q] or p in needed[q ^ 1]]
        far.append(lax.ppermute(cache, "queue", pairs))
        backs.append(by)
    far = jnp.concatenate(far, axis=0)
    near0 = lax.ppermute(
        cache, "queue", [(p, p ^ 1) for p in range(slots) if p in needed[p ^ 1]]
    )
    near1 = crossed(far, 1, "queue")
    caches = [cache, far, near0, near1]
    sources = (((0, 0),), tuple((0, b) for b in backs), ((1, 0),), tuple((1, b) for b in backs))

    first_facts = shifted(sums, STEPS)
    stride = 1
    while stride < lax.axis_size("mp"):
        got = crossed(first_facts, stride, "mp")
        first_facts = first_facts + got
        stride = 2 * stride
    second_facts = shifted(facts, STEPS - 1)
    landed = []
    for chunk in chunks:
        landed.append(shifted(chunk, STEPS))

    moved, partial, first_head = [], [], 0
    for part in landed:
        new, *partial = denoise(
            first_facts, sigma, group_len, first_facts, level_gain, [part], caches, sources,
            first_head, False, listed, partial,
        )
        first_head += part.shape[1] // HEAD_DIM
        moved.append(new)
    second_sums = lax.psum(partial[0], "mp")
    (out,) = denoise(
        second_facts, sigma, group_len, second_sums, level_gain, moved, caches, sources, 0, True, listed
    )
    return out


def solution(mesh):
    in_specs = (
        P("queue", None, "mp"),
        P("queue", None, "mp"),
        P("queue", None, "mp"),
        P(None, "mp"),
        P(),
        P("queue"),
        P(),
        P("queue", None),
        P("queue"),
    )
    out_specs = P("queue", None, "mp")

    return jax.shard_map(on_device, mesh=mesh, in_specs=in_specs, out_specs=out_specs, check_vma=False)
```
